512 devices in a mesh: row: 16 (over x_lo, y, core), col: 32 (over x_hi, z).
Axes of the slice: x: 4 (x_hi: 2, x_lo: 2; x = x_hi * 2 + x_lo), y: 4, z: 16, core: 2. Of those that a mesh axis runs over, the one named last changes fastest.
Arguments:
- inverse_slab: bfloat16 [65536, 8192], P('row', 'col'), may hold values from -0.0234375 to 0.0234375
- cot_solved: bfloat16 [64, 65536], P(None, ('row', 'col')), may hold values from -6 to 6
- cot_direct: bfloat16 [64, 8192], P(None, 'col'), may hold values from -6 to 6
- solved_panel: bfloat16 [64, 65536], P(None, 'col'), may hold values from -1.078125 to 1.078125
Outputs:
- grad_factor: float32 [64, 8192], P(None, 'col')
- grad_operator: bfloat16 [8192, 65536], P('row', 'col')
The draws below stay inside these ranges and needn't reach their ends.
All inputs are finite; a program needn't handle non-finite values.
Results may differ from the reference program's by a relative error of at most 0.0049.
Values may be sent and summed in bfloat16 or wider, within the bound.
No kernel may reach another device: no remote copies, remote signals or barrier semaphores. Data moves between devices by JAX's collectives and lax.ppermute only.
A program may use at most 64 MiB of HBM per device.

```python
import jax
import jax.numpy as jnp
from jax import lax

N = 65536
K = 64
W = 8192


def levels(stream_key, shape, pieces, low, top_value):
    gain = 1.0
    for axis_at, blocks in pieces:
        heights = jax.random.uniform(jax.random.fold_in(jax.random.fold_in(stream_key, 6), axis_at), (blocks,), jnp.float32, low / len(pieces), top_value / len(pieces))
        gain = gain * jnp.repeat(jnp.exp(heights), shape[axis_at] // blocks).reshape((-1,) + (1,) * (len(shape) - 1 - axis_at))
    return gain


def bell_draw(stream_key, shape, spread, bound, cuts=(), held_as=jnp.bfloat16):
    entries = jax.random.normal(stream_key, shape, jnp.float32) * spread
    if len(cuts) > 0:
        entries = levels(stream_key, shape, cuts, -0.22, 0.18) * entries
    return jnp.clip(entries, min=-bound, max=bound).astype(held_as)


def setup_inputs(seed: int = 0) -> dict:
    streams_of = jax.random.split(jax.random.key(seed), 5)
    inverse_slab = bell_draw(streams_of[0], (N, W), N ** -0.5, 0.0234375, ((0, 16), (1, 32)))
    cot_solved = bell_draw(streams_of[1], (K, N), 1.0, 6.0, ((1, 512),))
    cot_direct = bell_draw(streams_of[2], (K, W), 1.0, 6.0, ((1, 32),))
    solved_panel = bell_draw(streams_of[3], (K, N), 0.18, 1.078125, ((1, 32),))
    return dict(inverse_slab=inverse_slab, cot_solved=cot_solved, cot_direct=cot_direct, solved_panel=solved_panel)


def reference(inverse_slab, cot_solved, cot_direct, solved_panel):
    scale = 1.0 / jnp.sqrt(jnp.float32(2.0))
    pulled = jnp.dot(cot_solved, inverse_slab, preferred_element_type=jnp.float32)
    grad_factor = (cot_direct.astype(jnp.float32) + pulled) * scale
    pulled_low = pulled.astype(jnp.bfloat16)
    width = pulled_low.shape[1]
    block = min(width, 1024)
    blocks = pulled_low.reshape(pulled_low.shape[0], width // block, block).transpose(1, 0, 2)

    def one_block(piece):
        value = lax.dot_general(piece, solved_panel, (((0,), (0,)), ((), ())), preferred_element_type=jnp.float32)
        return (value * -scale).astype(jnp.bfloat16)
    grad_operator = lax.map(one_block, blocks).reshape(width, solved_panel.shape[1])
    return (grad_factor, grad_operator)
```

```python
import jax
import jax.numpy as jnp
from jax import lax
from jax.experimental import pallas as pl
from jax.experimental.pallas import tpu as pltpu
from jax.sharding import PartitionSpec as P

SUB, LANE = 8, 128
F32, BF16 = jnp.float32, jnp.bfloat16
VMEM = pltpu.VMEM


def full(shape):
    return pl.BlockSpec(shape, lambda *_: (0,) * len(shape))


def partial_kernel(blocks_ref, slab_ref, out_ref):
    n, _, b = blocks_ref.shape
    pair = 2
    total = None
    for i in range(0, n, pair):
        left = jnp.concatenate([blocks_ref[i + j] for j in range(pair)], axis=1)
        term = jnp.dot(left, slab_ref[i * b : (i + pair) * b, :], preferred_element_type=F32)
        total = term if total is None else total + term
    tiles_across = total.shape[1] // LANE
    for t in range(out_ref.shape[0]):
        i, j = t // tiles_across, t % tiles_across
        out_ref[t] = total[i * SUB : (i + 1) * SUB, j * LANE : (j + 1) * LANE]


def partial_tiles(blocks, slab):
    n, k, b = blocks.shape
    tiles = (k // SUB) * (slab.shape[1] // LANE)
    return pl.pallas_call(
        partial_kernel,
        out_shape=jax.ShapeDtypeStruct((tiles, SUB, LANE), F32),
        cost_estimate=pl.CostEstimate(
            flops=2 * n * k * b * slab.shape[1],
            bytes_accessed=2 * (blocks.size + slab.size) + 4 * tiles * SUB * LANE,
            transcendentals=0,
        ),
    )(blocks, slab)


def reduced_kernel(tiles_ref, high_ref, own_ref):
    pulled = tiles_ref[0]
    for t in range(1, tiles_ref.shape[0]):
        pulled = pulled + tiles_ref[t]
    high = pulled.astype(BF16)
    low = (pulled - high.astype(F32)).astype(BF16)
    for t in range(high_ref.shape[0]):
        high_ref[t] = high
    for t in range(own_ref.shape[0]):
        own_ref[t, 0] = high
        own_ref[t, 1] = low


def reduced(tiles, copies):
    rows = tiles.shape[0]
    tile = tiles.shape[1:]
    return pl.pallas_call(
        reduced_kernel,
        out_shape=[
            jax.ShapeDtypeStruct((copies,) + tile, BF16),
            jax.ShapeDtypeStruct((rows, 2) + tile, BF16),
        ],
        cost_estimate=pl.CostEstimate(
            flops=tiles.size, bytes_accessed=4 * tiles.size + 2 * (copies + 2 * rows) * SUB * LANE, transcendentals=0
        ),
    )(tiles)


def product_kernel(scale, tiles_ref, direct_ref, panel_ref, factor_ref, out_ref, left_ref):
    rows = tiles_ref.shape[0]
    width = direct_ref.shape[1]
    across = width // LANE
    chunk = out_ref.shape[0]

    @pl.when(pl.program_id(0) == 0)
    def _():
        for t in range(rows):
            i, j = t // across, t % across
            at = slice(i * SUB, (i + 1) * SUB)
            for b in range(2):
                lane = (b * across + j) * LANE
                left_ref[lane // chunk, at, lane % chunk : lane % chunk + LANE] = tiles_ref[t, b].astype(F32)
            lanes = slice(j * LANE, (j + 1) * LANE)
            pulled = tiles_ref[t, 2].astype(F32) + tiles_ref[t, 3].astype(F32)
            factor_ref[at, lanes] = (direct_ref[at, lanes].astype(F32) + pulled) * scale

    left = left_ref[pl.program_id(0)].astype(BF16)
    product = lax.dot_general(left, panel_ref[...], (((0,), (0,)), ((), ())), preferred_element_type=F32)
    out_ref[...] = (product * -scale).astype(BF16)


def products(tiles, direct, panel, scale):
    k, width = direct.shape
    depth = 2 * width
    chunk = depth // 4
    columns = panel.shape[1]

    def kernel(*refs):
        product_kernel(scale, *refs)

    return pl.pallas_call(
        kernel,
        grid=(depth // chunk,),
        in_specs=[full(tiles.shape), full(direct.shape), full(panel.shape)],
        out_specs=[full((k, width)), pl.BlockSpec((chunk, columns), lambda i: (i, 0))],
        out_shape=[
            jax.ShapeDtypeStruct((k, width), F32),
            jax.ShapeDtypeStruct((depth, columns), BF16),
        ],
        scratch_shapes=[VMEM((depth // chunk, k, chunk), F32)],
        cost_estimate=pl.CostEstimate(
            flops=2 * k * depth * columns,
            bytes_accessed=2 * (depth * columns + panel.size + tiles.size),
            transcendentals=0,
        ),
    )(tiles, direct, panel)


def body(inverse_slab, cot_solved, cot_direct, solved_panel):
    scale = 0.5 ** 0.5
    rows, cols = lax.axis_size("row"), lax.axis_size("col")
    blocks = lax.all_to_all(
        jnp.broadcast_to(cot_solved, (cols,) + cot_solved.shape), "col", 0, 0, tiled=True
    )
    tiles = partial_tiles(blocks, inverse_slab)
    high, own = reduced(lax.all_to_all(tiles, "row", 0, 0, tiled=True), cols)
    every = lax.all_to_all(high, "col", 0, 0, tiled=True)
    sent = jnp.concatenate([every.reshape((rows, cols // rows) + high.shape[1:]), own], axis=1)
    needed = lax.all_to_all(sent, "row", 0, 0, tiled=True)
    return tuple(products(needed, cot_direct, solved_panel, scale))


def solution(mesh):
    in_specs = (P("row", "col"), P(None, ("row", "col")), P(None, "col"), P(None, "col"))
    out_specs = (P(None, "col"), P("row", "col"))
    return jax.shard_map(body, mesh=mesh, in_specs=in_specs, out_specs=out_specs, check_vma=False)
```

```python
import jax
import jax.numpy as jnp
from jax import lax
from jax.experimental import pallas as pl
from jax.experimental.pallas import tpu as pltpu
from jax.sharding import Mesh, PartitionSpec as P

SUB, LANE = 8, 128
F32, BF16 = jnp.float32, jnp.bfloat16
COL = ("far", "near")
PARAMS = pltpu.CompilerParams(vmem_limit_bytes=8 << 20)


def full(shape):
    return pl.BlockSpec(shape, lambda *_: (0,) * len(shape))


def half_sum(parity, blocks_ref, slab_ref):
    pair = 2
    total = None
    for i in range(0, blocks_ref.shape[0], pair):
        left = jnp.concatenate([blocks_ref[i + j] for j in range(pair)], axis=1)
        right = jnp.concatenate([slab_ref[i + j, parity] for j in range(pair)], axis=0)
        term = jnp.dot(left, right, preferred_element_type=F32)
        total = term if total is None else total + term
    return total


def own_half_kernel(blocks_ref, slab_ref, out_ref):
    out_ref[...] = half_sum(lax.axis_index("near"), blocks_ref, slab_ref)


def other_half_kernel(blocks_ref, slab_ref, first_ref, out_ref):
    total = first_ref[...] + half_sum(1 - lax.axis_index("near"), blocks_ref, slab_ref)
    across = total.shape[1] // LANE
    for t in range(out_ref.shape[0]):
        i, j = t // across, t % across
        out_ref[t] = total[i * SUB : (i + 1) * SUB, j * LANE : (j + 1) * LANE]


def own_half(blocks, slab):
    n, k, b = blocks.shape
    width = slab.shape[-1]
    return pl.pallas_call(
        own_half_kernel,
        out_shape=jax.ShapeDtypeStruct((k, width), F32),
        compiler_params=PARAMS,
        cost_estimate=pl.CostEstimate(
            flops=2 * n * k * b * width, bytes_accessed=2 * blocks.size + slab.size, transcendentals=0
        ),
    )(blocks, slab)


def other_half(blocks, slab, first):
    n, k, b = blocks.shape
    width = slab.shape[-1]
    tiles = (k // SUB) * (width // LANE)
    return pl.pallas_call(
        other_half_kernel,
        out_shape=jax.ShapeDtypeStruct((tiles, SUB, LANE), F32),
        compiler_params=PARAMS,
        cost_estimate=pl.CostEstimate(
            flops=2 * n * k * b * width, bytes_accessed=2 * blocks.size + slab.size, transcendentals=0
        ),
    )(blocks, slab, first)


def reduced_kernel(tiles_ref, high_ref, own_ref):
    pulled = tiles_ref[0]
    for t in range(1, tiles_ref.shape[0]):
        pulled = pulled + tiles_ref[t]
    high = pulled.astype(BF16)
    low = (pulled - high.astype(F32)).astype(BF16)
    for t in range(high_ref.shape[0]):
        high_ref[t] = high
    for t in range(own_ref.shape[0]):
        own_ref[t, 0] = high
        own_ref[t, 1] = low


def reduced(tiles, copies):
    rows = tiles.shape[0]
    tile = tiles.shape[1:]
    return pl.pallas_call(
        reduced_kernel,
        out_shape=[jax.ShapeDtypeStruct((copies,) + tile, BF16), jax.ShapeDtypeStruct((rows, 2) + tile, BF16)],
        compiler_params=PARAMS,
        cost_estimate=pl.CostEstimate(flops=tiles.size, bytes_accessed=10 * tiles.size, transcendentals=0),
    )(tiles)


def product_kernel(scale, tiles_ref, direct_ref, panel_ref, factor_ref, out_ref, left_ref):
    rows, blocks = tiles_ref.shape[0], tiles_ref.shape[1] - 2
    across = direct_ref.shape[1] // LANE
    chunk = out_ref.shape[0]

    @pl.when(pl.program_id(0) == 0)
    def _():
        for t in range(rows):
            i, j = t // across, t % across
            at = slice(i * SUB, (i + 1) * SUB)
            for b in range(blocks):
                lane = (b * across + j) * LANE
                left_ref[lane // chunk, at, lane % chunk : lane % chunk + LANE] = tiles_ref[t, b].astype(F32)
            lanes = slice(j * LANE, (j + 1) * LANE)
            pulled = tiles_ref[t, blocks].astype(F32) + tiles_ref[t, blocks + 1].astype(F32)
            factor_ref[at, lanes] = (direct_ref[at, lanes].astype(F32) + pulled) * scale

    left = left_ref[pl.program_id(0)].astype(BF16)
    product = lax.dot_general(left, panel_ref[...], (((0,), (0,)), ((), ())), preferred_element_type=F32)
    out_ref[...] = (product * -scale).astype(BF16)


def products(tiles, direct, panel, scale):
    k, columns = panel.shape
    depth = (tiles.shape[1] - 2) * direct.shape[1]
    chunk = depth // 4

    def kernel(*refs):
        product_kernel(scale, *refs)

    return pl.pallas_call(
        kernel,
        grid=(depth // chunk,),
        in_specs=[full(tiles.shape), full(direct.shape), full(panel.shape)],
        out_specs=[full(direct.shape), pl.BlockSpec((chunk, columns), lambda i: (i, 0))],
        out_shape=[jax.ShapeDtypeStruct(direct.shape, F32), jax.ShapeDtypeStruct((depth, columns), BF16)],
        scratch_shapes=[pltpu.VMEM((depth // chunk, k, chunk), F32)],
        compiler_params=PARAMS,
        cost_estimate=pl.CostEstimate(
            flops=2 * k * depth * columns, bytes_accessed=2 * (depth * columns + panel.size), transcendentals=0
        ),
    )(tiles, direct, panel)


def exchange(x, axes):
    return lax.all_to_all(x, axes, 0, 0, tiled=True)


def body(inverse_slab, cot_solved, cot_direct, solved_panel):
    scale = 0.5 ** 0.5
    rows, far, near = (lax.axis_size(a) for a in ("row",) + COL)
    slab = inverse_slab.reshape(far, near, cot_solved.shape[1], inverse_slab.shape[1])
    mine = exchange(jnp.broadcast_to(cot_solved, (far,) + cot_solved.shape), "far")
    theirs = lax.ppermute(mine, "near", [(0, 1), (1, 0)])
    tiles = other_half(theirs, slab, own_half(mine, slab))
    high, own = reduced(exchange(tiles, "row"), far * near)
    every = exchange(high, COL).reshape((rows, far * near // rows) + high.shape[1:])
    needed = exchange(jnp.concatenate([every, own], axis=1), "row")
    return tuple(products(needed, cot_direct, solved_panel, scale))


def solution(mesh):
    near = 2
    rows, cols = mesh.devices.shape
    fine = Mesh(mesh.devices.reshape(rows, cols // near, near), ("row",) + COL)
    in_specs = (P("row", COL), P(None, ("row",) + COL), P(None, COL), P(None, COL))
    out_specs = (P(None, COL), P("row", COL))
    return jax.shard_map(body, mesh=fine, in_specs=in_specs, out_specs=out_specs, check_vma=False)
```

```python
import jax
import jax.numpy as jnp
from jax import lax
from jax.experimental import pallas as pl
from jax.experimental.pallas import tpu as pltpu
from jax.sharding import Mesh, PartitionSpec as P

SUB, LANE = 8, 128
F32, BF16 = jnp.float32, jnp.bfloat16
COL = ("half", "far", "near")
CLOSE = ("half", "near")
PARAMS = pltpu.CompilerParams(vmem_limit_bytes=8 << 20)


def full(shape):
    return pl.BlockSpec(shape, lambda *_: (0,) * len(shape))


def share_sum(half, near, blocks_ref, slab_ref, lead=()):
    pair = 2
    total = None
    for i in range(0, slab_ref.shape[1], pair):
        left = jnp.concatenate([blocks_ref[lead + (i + j,)] for j in range(pair)], axis=1)
        right = jnp.concatenate([slab_ref[half, i + j, near] for j in range(pair)], axis=0)
        term = jnp.dot(left, right, preferred_element_type=F32)
        total = term if total is None else total + term
    return total


def own_share_kernel(blocks_ref, slab_ref, out_ref):
    out_ref[...] = share_sum(lax.axis_index("half"), lax.axis_index("near"), blocks_ref, slab_ref)


def other_shares_kernel(blocks_ref, slab_ref, first_ref, out_ref):
    halves, _, nears = slab_ref.shape[:3]
    half, near = lax.axis_index("half"), lax.axis_index("near")
    total = first_ref[...]
    for dh in range(halves):
        for dn in range(nears):
            if dh or dn:
                h, n = lax.rem(half + dh, halves), lax.rem(near + dn, nears)
                total = total + share_sum(h, n, blocks_ref, slab_ref, (h * nears + n,))
    across = total.shape[1] // LANE
    for t in range(out_ref.shape[0]):
        i, j = t // across, t % across
        out_ref[t] = total[i * SUB : (i + 1) * SUB, j * LANE : (j + 1) * LANE]


def own_share(blocks, slab):
    n, k, b = blocks.shape
    width = slab.shape[-1]
    return pl.pallas_call(
        own_share_kernel,
        out_shape=jax.ShapeDtypeStruct((k, width), F32),
        compiler_params=PARAMS,
        cost_estimate=pl.CostEstimate(
            flops=2 * n * k * b * width, bytes_accessed=2 * (blocks.size + n * b * width), transcendentals=0
        ),
    )(blocks, slab)


def other_shares(blocks, slab, first):
    shares, n, k, b = blocks.shape
    width = slab.shape[-1]
    tiles = (k // SUB) * (width // LANE)
    return pl.pallas_call(
        other_shares_kernel,
        out_shape=jax.ShapeDtypeStruct((tiles, SUB, LANE), F32),
        compiler_params=PARAMS,
        cost_estimate=pl.CostEstimate(
            flops=2 * shares * n * k * b * width, bytes_accessed=2 * (blocks.size + slab.size), transcendentals=0
        ),
    )(blocks, slab, first)


def reduced_kernel(tiles_ref, high_ref, own_ref):
    pulled = tiles_ref[0]
    for t in range(1, tiles_ref.shape[0]):
        pulled = pulled + tiles_ref[t]
    high = pulled.astype(BF16)
    low = (pulled - high.astype(F32)).astype(BF16)
    for t in range(high_ref.shape[0]):
        high_ref[t] = high
    for t in range(own_ref.shape[0]):
        own_ref[t, 0] = high
        own_ref[t, 1] = low


def reduced(tiles, copies):
    rows = tiles.shape[0]
    tile = tiles.shape[1:]
    return pl.pallas_call(
        reduced_kernel,
        out_shape=[jax.ShapeDtypeStruct((copies,) + tile, BF16), jax.ShapeDtypeStruct((rows, 2) + tile, BF16)],
        compiler_params=PARAMS,
        cost_estimate=pl.CostEstimate(flops=tiles.size, bytes_accessed=10 * tiles.size, transcendentals=0),
    )(tiles)


def product_kernel(scale, tiles_ref, direct_ref, panel_ref, factor_ref, out_ref, left_ref):
    rows, blocks = tiles_ref.shape[0], tiles_ref.shape[1] - 2
    across = direct_ref.shape[1] // LANE
    chunk = out_ref.shape[0]

    @pl.when(pl.program_id(0) == 0)
    def _():
        for t in range(rows):
            i, j = t // across, t % across
            at = slice(i * SUB, (i + 1) * SUB)
            for b in range(blocks):
                lane = (b * across + j) * LANE
                left_ref[lane // chunk, at, lane % chunk : lane % chunk + LANE] = tiles_ref[t, b].astype(F32)
            lanes = slice(j * LANE, (j + 1) * LANE)
            pulled = tiles_ref[t, blocks].astype(F32) + tiles_ref[t, blocks + 1].astype(F32)
            factor_ref[at, lanes] = (direct_ref[at, lanes].astype(F32) + pulled) * scale

    left = left_ref[pl.program_id(0)].astype(BF16)
    product = lax.dot_general(left, panel_ref[...], (((0,), (0,)), ((), ())), preferred_element_type=F32)
    out_ref[...] = (product * -scale).astype(BF16)


def products(tiles, direct, panel, scale):
    k, columns = panel.shape
    depth = (tiles.shape[1] - 2) * direct.shape[1]
    chunk = depth // 4

    def kernel(*refs):
        product_kernel(scale, *refs)

    return pl.pallas_call(
        kernel,
        grid=(depth // chunk,),
        in_specs=[full(tiles.shape), full(direct.shape), full(panel.shape)],
        out_specs=[full(direct.shape), pl.BlockSpec((chunk, columns), lambda i: (i, 0))],
        out_shape=[jax.ShapeDtypeStruct(direct.shape, F32), jax.ShapeDtypeStruct((depth, columns), BF16)],
        scratch_shapes=[pltpu.VMEM((depth // chunk, k, chunk), F32)],
        compiler_params=PARAMS,
        cost_estimate=pl.CostEstimate(
            flops=2 * k * depth * columns, bytes_accessed=2 * (depth * columns + panel.size), transcendentals=0
        ),
    )(tiles, direct, panel)


def exchange(x, axes):
    return lax.all_to_all(x, axes, 0, 0, tiled=True)


def body(inverse_slab, cot_solved, cot_direct, solved_panel):
    scale = 0.5 ** 0.5
    rows, half, far, near = (lax.axis_size(a) for a in ("row",) + COL)
    cols = half * far * near
    slab = inverse_slab.reshape(half, far, near, cot_solved.shape[1], inverse_slab.shape[1])
    mine = exchange(jnp.broadcast_to(cot_solved, (far,) + cot_solved.shape), "far")
    shares = exchange(jnp.broadcast_to(mine, (half * near,) + mine.shape), CLOSE)
    tiles = other_shares(shares, slab, own_share(mine, slab))
    high, own = reduced(exchange(tiles, "row"), cols)
    every = exchange(high, COL).reshape((rows, cols // rows) + high.shape[1:])
    needed = exchange(jnp.concatenate([every, own], axis=1), "row")
    return tuple(products(needed, cot_direct, solved_panel, scale))


def solution(mesh):
    half, near = 2, 2
    rows, cols = mesh.devices.shape
    fine = Mesh(mesh.devices.reshape(rows, half, cols // (half * near), near), ("row",) + COL)
    in_specs = (P("row", COL), P(None, ("row",) + COL), P(None, COL), P(None, COL))
    out_specs = (P(None, COL), P("row", COL))
    return jax.shard_map(body, mesh=fine, in_specs=in_specs, out_specs=out_specs, check_vma=False)
```

```python
import jax
import jax.numpy as jnp
from jax import lax
from jax.experimental import pallas as pl
from jax.experimental.pallas import tpu as pltpu
from jax.sharding import Mesh, PartitionSpec as P

SUB, LANE = 8, 128
F32, BF16 = jnp.float32, jnp.bfloat16
COL = ("half", "far", "near")
CLOSE = ("half", "near")
PARAMS = pltpu.CompilerParams(vmem_limit_bytes=8 << 20)


def share_sum(half, near, blocks_ref, slab_ref, lead=()):
    pair = 2
    total = None
    for i in range(0, slab_ref.shape[1], pair):
        left = jnp.concatenate([blocks_ref[lead + (i + j,)] for j in range(pair)], axis=1)
        right = jnp.concatenate([slab_ref[half, i + j, near] for j in range(pair)], axis=0)
        term = jnp.dot(left, right, preferred_element_type=F32)
        total = term if total is None else total + term
    return total


def own_share_kernel(blocks_ref, slab_ref, out_ref):
    out_ref[...] = share_sum(lax.axis_index("half"), lax.axis_index("near"), blocks_ref, slab_ref)


def other_shares_kernel(blocks_ref, slab_ref, first_ref, out_ref):
    halves, _, nears = slab_ref.shape[:3]
    half, near = lax.axis_index("half"), lax.axis_index("near")
    total = first_ref[...]
    for dh in range(halves):
        for dn in range(nears):
            if dh or dn:
                h, n = lax.rem(half + dh, halves), lax.rem(near + dn, nears)
                total = total + share_sum(h, n, blocks_ref, slab_ref, (h * nears + n,))
    across = total.shape[1] // LANE
    for t in range(out_ref.shape[0]):
        i, j = t // across, t % across
        out_ref[t] = total[i * SUB : (i + 1) * SUB, j * LANE : (j + 1) * LANE]


def own_share(blocks, slab):
    n, k, b = blocks.shape
    width = slab.shape[-1]
    return pl.pallas_call(
        own_share_kernel,
        out_shape=jax.ShapeDtypeStruct((k, width), F32),
        compiler_params=PARAMS,
        cost_estimate=pl.CostEstimate(
            flops=2 * n * k * b * width, bytes_accessed=2 * (blocks.size + n * b * width), transcendentals=0
        ),
    )(blocks, slab)


def other_shares(blocks, slab, first):
    shares, n, k, b = blocks.shape
    width = slab.shape[-1]
    tiles = (k // SUB) * (width // LANE)
    return pl.pallas_call(
        other_shares_kernel,
        out_shape=jax.ShapeDtypeStruct((tiles, SUB, LANE), F32),
        compiler_params=PARAMS,
        cost_estimate=pl.CostEstimate(
            flops=2 * shares * n * k * b * width, bytes_accessed=2 * (blocks.size + slab.size), transcendentals=0
        ),
    )(blocks, slab, first)


def reduced_kernel(tiles_ref, high_ref, own_ref):
    pulled = tiles_ref[0]
    for t in range(1, tiles_ref.shape[0]):
        pulled = pulled + tiles_ref[t]
    high = pulled.astype(BF16)
    low = (pulled - high.astype(F32)).astype(BF16)
    for t in range(high_ref.shape[0]):
        high_ref[t] = high
    for t in range(own_ref.shape[0]):
        own_ref[t, 0] = high
        own_ref[t, 1] = low


def reduced(tiles, copies):
    rows = tiles.shape[0]
    tile = tiles.shape[1:]
    return pl.pallas_call(
        reduced_kernel,
        out_shape=[jax.ShapeDtypeStruct((copies,) + tile, BF16), jax.ShapeDtypeStruct((rows, 2) + tile, BF16)],
        compiler_params=PARAMS,
        cost_estimate=pl.CostEstimate(flops=tiles.size, bytes_accessed=10 * tiles.size, transcendentals=0),
    )(tiles)


def product_kernel(scale, tiles_ref, direct_ref, panel_ref, factor_ref, out_ref, left_ref, sum_ref, wide_ref, sems):
    rows, blocks = tiles_ref.shape[0], tiles_ref.shape[1] - 2
    across = direct_ref.shape[1] // LANE
    chunks = sems.shape[0] - 1
    chunk = out_ref.shape[0] // chunks
    for t in range(rows):
        i, j = t // across, t % across
        at = slice(i * SUB, (i + 1) * SUB)
        for b in range(blocks):
            lane = (b * across + j) * LANE
            left_ref[at, lane : lane + LANE] = tiles_ref[t, b].astype(F32)
        lanes = slice(j * LANE, (j + 1) * LANE)
        pulled = tiles_ref[t, blocks].astype(F32) + tiles_ref[t, blocks + 1].astype(F32)
        sum_ref[at, lanes] = (direct_ref[at, lanes].astype(F32) + pulled) * scale
    copies = [pltpu.make_async_copy(sum_ref, factor_ref, sems.at[chunks])]
    copies[0].start()
    for c in range(chunks):
        at = slice(c * chunk, (c + 1) * chunk)
        left = left_ref[:, at].astype(BF16)
        product = lax.dot_general(left, panel_ref[...], (((0,), (0,)), ((), ())), preferred_element_type=F32)
        wide_ref[at] = (product * -scale).astype(BF16)
        copies.append(pltpu.make_async_copy(wide_ref.at[at], out_ref.at[at], sems.at[c]))
        copies[-1].start()
    for copy in copies:
        copy.wait()


def products(tiles, direct, panel, scale):
    k, columns = panel.shape
    depth = (tiles.shape[1] - 2) * direct.shape[1]
    chunks = 4

    def kernel(*refs):
        product_kernel(scale, *refs)

    return pl.pallas_call(
        kernel,
        in_specs=[pl.BlockSpec(memory_space=pltpu.VMEM)] * 3,
        out_specs=[pl.BlockSpec(memory_space=pl.ANY)] * 2,
        out_shape=[jax.ShapeDtypeStruct(direct.shape, F32), jax.ShapeDtypeStruct((depth, columns), BF16)],
        scratch_shapes=[
            pltpu.VMEM((k, depth), F32),
            pltpu.VMEM(direct.shape, F32),
            pltpu.VMEM((depth, columns), BF16),
            pltpu.SemaphoreType.DMA((chunks + 1,)),
        ],
        compiler_params=PARAMS,
        cost_estimate=pl.CostEstimate(
            flops=2 * k * depth * columns, bytes_accessed=2 * (depth * columns + panel.size), transcendentals=0
        ),
    )(tiles, direct, panel)


def copies_kernel(x_ref, out_ref):
    for i in range(out_ref.shape[0]):
        out_ref[i] = x_ref[...]


def copies(x, n):
    return pl.pallas_call(
        copies_kernel,
        out_shape=jax.ShapeDtypeStruct((n,) + x.shape, x.dtype),
        compiler_params=PARAMS,
        cost_estimate=pl.CostEstimate(flops=0, bytes_accessed=2 * (n + 1) * x.size, transcendentals=0),
    )(x)


def exchange(x, axes):
    return lax.all_to_all(x, axes, 0, 0, tiled=True)


def body(inverse_slab, cot_solved, cot_direct, solved_panel):
    scale = 0.5 ** 0.5
    rows, half, far, near = (lax.axis_size(a) for a in ("row",) + COL)
    cols = half * far * near
    slab = inverse_slab.reshape(half, far, near, cot_solved.shape[1], inverse_slab.shape[1])
    mine = exchange(copies(cot_solved, far), "far")
    shares = exchange(copies(mine, half * near), CLOSE)
    tiles = other_shares(shares, slab, own_share(mine, slab))
    high, own = reduced(exchange(tiles, "row"), cols)
    every = exchange(high, COL).reshape((rows, cols // rows) + high.shape[1:])
    needed = exchange(jnp.concatenate([every, own], axis=1), "row")
    return tuple(products(needed, cot_direct, solved_panel, scale))


def solution(mesh):
    half, near = 2, 2
    rows, cols = mesh.devices.shape
    fine = Mesh(mesh.devices.reshape(rows, half, cols // (half * near), near), ("row",) + COL)
    in_specs = (P("row", COL), P(None, ("row",) + COL), P(None, COL), P(None, COL))
    out_specs = (P(None, COL), P("row", COL))
    return jax.shard_map(body, mesh=fine, in_specs=in_specs, out_specs=out_specs, check_vma=False)
```

```python
import jax
import jax.numpy as jnp
from jax import lax
from jax.experimental import pallas as pl
from jax.experimental.pallas import tpu as pltpu
from jax.sharding import Mesh, PartitionSpec as P

SUB, LANE = 8, 128
F32, BF16 = jnp.float32, jnp.bfloat16
COL = ("half", "far", "near")
CLOSE = ("half", "near")
PARAMS = pltpu.CompilerParams(vmem_limit_bytes=8 << 20)


def partial_kernel(blocks_ref, slab_ref, out_ref):
    halves, n, nears = slab_ref.shape[:3]
    total = None
    for h in range(halves):
        for i in range(n):
            left = jnp.concatenate([blocks_ref[h * nears + m, i] for m in range(nears)], axis=1)
            right = jnp.concatenate([slab_ref[h, i, m] for m in range(nears)], axis=0)
            term = jnp.dot(left, right, preferred_element_type=F32)
            total = term if total is None else total + term
    across = total.shape[1] // LANE
    for t in range(out_ref.shape[0]):
        i, j = t // across, t % across
        out_ref[t] = total[i * SUB : (i + 1) * SUB, j * LANE : (j + 1) * LANE]


def partial_tiles(blocks, slab):
    shares, n, k, b = blocks.shape
    width = slab.shape[-1]
    tiles = (k // SUB) * (width // LANE)
    return pl.pallas_call(
        partial_kernel,
        out_shape=jax.ShapeDtypeStruct((tiles, SUB, LANE), F32),
        compiler_params=PARAMS,
        cost_estimate=pl.CostEstimate(
            flops=2 * shares * n * k * b * width, bytes_accessed=2 * (blocks.size + slab.size), transcendentals=0
        ),
    )(blocks, slab)


def reduced_kernel(tiles_ref, high_ref, own_ref):
    pulled = tiles_ref[0]
    for t in range(1, tiles_ref.shape[0]):
        pulled = pulled + tiles_ref[t]
    high = pulled.astype(BF16)
    low = (pulled - high.astype(F32)).astype(BF16)
    for t in range(high_ref.shape[0]):
        high_ref[t] = high
    for t in range(own_ref.shape[0]):
        own_ref[t, 0] = high
        own_ref[t, 1] = low


def reduced(tiles, copies):
    rows = tiles.shape[0]
    tile = tiles.shape[1:]
    return pl.pallas_call(
        reduced_kernel,
        out_shape=[jax.ShapeDtypeStruct((copies,) + tile, BF16), jax.ShapeDtypeStruct((rows, 2) + tile, BF16)],
        compiler_params=PARAMS,
        cost_estimate=pl.CostEstimate(flops=tiles.size, bytes_accessed=10 * tiles.size, transcendentals=0),
    )(tiles)


def product_kernel(scale, tiles_ref, direct_ref, panel_ref, factor_ref, out_ref, left_ref, sum_ref, wide_ref, sems):
    rows, blocks = tiles_ref.shape[0], tiles_ref.shape[1] - 2
    across = direct_ref.shape[1] // LANE
    chunks = sems.shape[0] - 1
    chunk = out_ref.shape[0] // chunks
    for t in range(rows):
        i, j = t // across, t % across
        at = slice(i * SUB, (i + 1) * SUB)
        for b in range(blocks):
            lane = (b * across + j) * LANE
            left_ref[at, lane : lane + LANE] = tiles_ref[t, b].astype(F32)
        lanes = slice(j * LANE, (j + 1) * LANE)
        pulled = tiles_ref[t, blocks].astype(F32) + tiles_ref[t, blocks + 1].astype(F32)
        sum_ref[at, lanes] = (direct_ref[at, lanes].astype(F32) + pulled) * scale
    copies = [pltpu.make_async_copy(sum_ref, factor_ref, sems.at[chunks])]
    copies[0].start()
    for c in range(chunks):
        at = slice(c * chunk, (c + 1) * chunk)
        left = left_ref[:, at].astype(BF16)
        product = lax.dot_general(left, panel_ref[...], (((0,), (0,)), ((), ())), preferred_element_type=F32)
        wide_ref[at] = (product * -scale).astype(BF16)
        copies.append(pltpu.make_async_copy(wide_ref.at[at], out_ref.at[at], sems.at[c]))
        copies[-1].start()
    for copy in copies:
        copy.wait()


def products(tiles, direct, panel, scale):
    k, columns = panel.shape
    depth = (tiles.shape[1] - 2) * direct.shape[1]
    chunks = 4

    def kernel(*refs):
        product_kernel(scale, *refs)

    return pl.pallas_call(
        kernel,
        in_specs=[pl.BlockSpec(memory_space=pltpu.VMEM)] * 3,
        out_specs=[pl.BlockSpec(memory_space=pl.ANY)] * 2,
        out_shape=[jax.ShapeDtypeStruct(direct.shape, F32), jax.ShapeDtypeStruct((depth, columns), BF16)],
        scratch_shapes=[
            pltpu.VMEM((k, depth), F32),
            pltpu.VMEM(direct.shape, F32),
            pltpu.VMEM((depth, columns), BF16),
            pltpu.SemaphoreType.DMA((chunks + 1,)),
        ],
        compiler_params=PARAMS,
        cost_estimate=pl.CostEstimate(
            flops=2 * k * depth * columns, bytes_accessed=2 * (depth * columns + panel.size), transcendentals=0
        ),
    )(tiles, direct, panel)


def copies_kernel(x_ref, out_ref):
    for i in range(out_ref.shape[0]):
        out_ref[i] = x_ref[...]


def fetched_copies_kernel(x_ref, out_ref, sems):
    fetches = [pltpu.make_async_copy(x_ref, out_ref.at[i], sems.at[i]) for i in range(out_ref.shape[0])]
    for fetch in fetches:
        fetch.start()
    for fetch in fetches:
        fetch.wait()


def fetched_copies(x, n):
    return pl.pallas_call(
        fetched_copies_kernel,
        in_specs=[pl.BlockSpec(memory_space=pltpu.HBM)],
        out_specs=pl.BlockSpec(memory_space=pltpu.VMEM),
        out_shape=jax.ShapeDtypeStruct((n,) + x.shape, x.dtype),
        scratch_shapes=[pltpu.SemaphoreType.DMA((n,))],
        compiler_params=PARAMS,
        cost_estimate=pl.CostEstimate(flops=0, bytes_accessed=4 * n * x.size, transcendentals=0),
    )(x)


def copies(x, n):
    return pl.pallas_call(
        copies_kernel,
        out_shape=jax.ShapeDtypeStruct((n,) + x.shape, x.dtype),
        compiler_params=PARAMS,
        cost_estimate=pl.CostEstimate(flops=0, bytes_accessed=2 * (n + 1) * x.size, transcendentals=0),
    )(x)


def exchange(x, axes):
    return lax.all_to_all(x, axes, 0, 0, tiled=True)


def body(inverse_slab, cot_solved, cot_direct, solved_panel):
    scale = 0.5 ** 0.5
    rows, half, far, near = (lax.axis_size(a) for a in ("row",) + COL)
    cols = half * far * near
    slab = inverse_slab.reshape(half, far, near, cot_solved.shape[1], inverse_slab.shape[1])
    mine = exchange(fetched_copies(pltpu.with_memory_space_constraint(cot_solved, pltpu.HBM), far), "far")
    shares = exchange(copies(mine, half * near), CLOSE)
    tiles = partial_tiles(shares, slab)
    high, own = reduced(exchange(tiles, "row"), cols)
    every = exchange(high, COL).reshape((rows, cols // rows) + high.shape[1:])
    needed = exchange(jnp.concatenate([every, own], axis=1), "row")
    return tuple(products(needed, cot_direct, solved_panel, scale))


def solution(mesh):
    half, near = 2, 2
    rows, cols = mesh.devices.shape
    fine = Mesh(mesh.devices.reshape(rows, half, cols // (half * near), near), ("row",) + COL)
    in_specs = (P("row", COL), P(None, ("row",) + COL), P(None, COL), P(None, COL))
    out_specs = (P(None, COL), P("row", COL))
    return jax.shard_map(body, mesh=fine, in_specs=in_specs, out_specs=out_specs, check_vma=False)
```

```python
import math

import jax
import jax.numpy as jnp
import numpy as np
from jax import lax
from jax.experimental import pallas as pl
from jax.experimental.pallas import tpu as pltpu
from jax.sharding import Mesh, PartitionSpec as P

SUB, LANE = 8, 128
F32, BF16 = jnp.float32, jnp.bfloat16
FAR = ("z3", "z2", "z1")
COL = ("half",) + FAR + ("near",)
CLOSE = ("half", "near")
SPREAD = ("near", "z1", "z2", "z3", "half")
PARAMS = pltpu.CompilerParams(vmem_limit_bytes=8 << 20)


def partial_kernel(blocks_ref, slab_ref, out_ref):
    halves, n, nears = slab_ref.shape[:3]
    total = None
    for h in range(halves):
        for i in range(n):
            left = jnp.concatenate([blocks_ref[h * nears + m, i] for m in range(nears)], axis=1)
            right = jnp.concatenate([slab_ref[h, i, m] for m in range(nears)], axis=0)
            term = jnp.dot(left, right, preferred_element_type=F32)
            total = term if total is None else total + term
    across = total.shape[1] // LANE
    for t in range(out_ref.shape[0]):
        i, j = t // across, t % across
        out_ref[t] = total[i * SUB : (i + 1) * SUB, j * LANE : (j + 1) * LANE]


def partial_tiles(blocks, slab):
    shares, n, k, b = blocks.shape
    width = slab.shape[-1]
    tiles = (k // SUB) * (width // LANE)
    return pl.pallas_call(
        partial_kernel,
        out_shape=jax.ShapeDtypeStruct((tiles, SUB, LANE), F32),
        compiler_params=PARAMS,
        cost_estimate=pl.CostEstimate(
            flops=2 * shares * n * k * b * width, bytes_accessed=2 * (blocks.size + slab.size), transcendentals=0
        ),
    )(blocks, slab)


def reduced_kernel(tiles_ref, high_ref, own_ref):
    pulled = tiles_ref[0]
    for t in range(1, tiles_ref.shape[0]):
        pulled = pulled + tiles_ref[t]
    high = pulled.astype(BF16)
    low = (pulled - high.astype(F32)).astype(BF16)
    for t in range(high_ref.shape[0]):
        high_ref[t] = high
    for t in range(own_ref.shape[0]):
        own_ref[t, 0] = high
        own_ref[t, 1] = low


def reduced(tiles, copies):
    rows = tiles.shape[0]
    tile = tiles.shape[1:]
    return pl.pallas_call(
        reduced_kernel,
        out_shape=[jax.ShapeDtypeStruct((copies,) + tile, BF16), jax.ShapeDtypeStruct((rows, 2) + tile, BF16)],
        compiler_params=PARAMS,
        cost_estimate=pl.CostEstimate(flops=tiles.size, bytes_accessed=10 * tiles.size, transcendentals=0),
    )(tiles)


def product_kernel(scale, tiles_ref, direct_ref, panel_ref, factor_ref, out_ref, left_ref, sum_ref, wide_ref, sems):
    rows, blocks = tiles_ref.shape[0], tiles_ref.shape[1] - 2
    across = direct_ref.shape[1] // LANE
    chunks = sems.shape[0] - 1
    chunk = out_ref.shape[0] // chunks
    for t in range(rows):
        i, j = t // across, t % across
        at = slice(i * SUB, (i + 1) * SUB)
        for b in range(blocks):
            lane = (b * across + j) * LANE
            left_ref[at, lane : lane + LANE] = tiles_ref[t, b].astype(F32)
        lanes = slice(j * LANE, (j + 1) * LANE)
        pulled = tiles_ref[t, blocks].astype(F32) + tiles_ref[t, blocks + 1].astype(F32)
        sum_ref[at, lanes] = (direct_ref[at, lanes].astype(F32) + pulled) * scale
    copies = [pltpu.make_async_copy(sum_ref, factor_ref, sems.at[chunks])]
    copies[0].start()
    for c in range(chunks):
        at = slice(c * chunk, (c + 1) * chunk)
        left = left_ref[:, at].astype(BF16)
        product = lax.dot_general(left, panel_ref[...], (((0,), (0,)), ((), ())), preferred_element_type=F32)
        wide_ref[at] = (product * -scale).astype(BF16)
        copies.append(pltpu.make_async_copy(wide_ref.at[at], out_ref.at[at], sems.at[c]))
        copies[-1].start()
    for copy in copies:
        copy.wait()


def products(tiles, direct, panel, scale):
    k, columns = panel.shape
    depth = (tiles.shape[1] - 2) * direct.shape[1]
    chunks = 4

    def kernel(*refs):
        product_kernel(scale, *refs)

    return pl.pallas_call(
        kernel,
        in_specs=[pl.BlockSpec(memory_space=pltpu.VMEM)] * 3,
        out_specs=[pl.BlockSpec(memory_space=pl.ANY)] * 2,
        out_shape=[jax.ShapeDtypeStruct(direct.shape, F32), jax.ShapeDtypeStruct((depth, columns), BF16)],
        scratch_shapes=[
            pltpu.VMEM((k, depth), F32),
            pltpu.VMEM(direct.shape, F32),
            pltpu.VMEM((depth, columns), BF16),
            pltpu.SemaphoreType.DMA((chunks + 1,)),
        ],
        compiler_params=PARAMS,
        cost_estimate=pl.CostEstimate(
            flops=2 * k * depth * columns, bytes_accessed=2 * (depth * columns + panel.size), transcendentals=0
        ),
    )(tiles, direct, panel)


def copies_kernel(x_ref, out_ref):
    for i in range(out_ref.shape[0]):
        out_ref[i] = x_ref[...]


def fetched_copies_kernel(x_ref, out_ref, sem):
    fetch = pltpu.make_async_copy(x_ref, out_ref.at[0], sem)
    fetch.start()
    fetch.wait()
    for i in range(1, out_ref.shape[0]):
        out_ref[i] = out_ref[0]


def fetched_copies(x, n):
    return pl.pallas_call(
        fetched_copies_kernel,
        in_specs=[pl.BlockSpec(memory_space=pltpu.HBM)],
        out_specs=pl.BlockSpec(memory_space=pltpu.VMEM),
        out_shape=jax.ShapeDtypeStruct((n,) + x.shape, x.dtype),
        scratch_shapes=[pltpu.SemaphoreType.DMA],
        compiler_params=PARAMS,
        cost_estimate=pl.CostEstimate(flops=0, bytes_accessed=4 * n * x.size, transcendentals=0),
    )(pltpu.with_memory_space_constraint(x, pltpu.HBM))


def joined_kernel(order, every_ref, own_ref, out_ref):
    rows, blocks = out_ref.shape[0], out_ref.shape[1] - own_ref.shape[1]
    for t in range(rows):
        for b in range(blocks):
            out_ref[t, b] = every_ref[order[t * blocks + b]]
        out_ref[t, blocks:] = own_ref[t]


def joined(order, every, own):
    rows = own.shape[0]
    blocks = every.shape[0] // rows

    def kernel(*refs):
        joined_kernel(order, *refs)

    shape = (rows, blocks + own.shape[1]) + own.shape[2:]
    return pl.pallas_call(
        kernel,
        out_shape=jax.ShapeDtypeStruct(shape, own.dtype),
        compiler_params=PARAMS,
        cost_estimate=pl.CostEstimate(flops=0, bytes_accessed=4 * (every.size + own.size), transcendentals=0),
    )(every, own)


def copies(x, n):
    return pl.pallas_call(
        copies_kernel,
        out_shape=jax.ShapeDtypeStruct((n,) + x.shape, x.dtype),
        compiler_params=PARAMS,
        cost_estimate=pl.CostEstimate(flops=0, bytes_accessed=2 * (n + 1) * x.size, transcendentals=0),
    )(x)


def exchange(x, axes):
    return lax.all_to_all(x, axes, 0, 0, tiled=True)


def places(sizes):
    grid = np.arange(math.prod(sizes.values())).reshape([sizes[a] for a in SPREAD])
    return grid.transpose([SPREAD.index(a) for a in COL]).reshape(-1).tolist()


def body(inverse_slab, cot_solved, cot_direct, solved_panel):
    scale = 0.5 ** 0.5
    sizes = {a: lax.axis_size(a) for a in COL}
    half, near = sizes["half"], sizes["near"]
    far = math.prod(sizes[a] for a in FAR)
    slab = inverse_slab.reshape(half, far, near, cot_solved.shape[1], inverse_slab.shape[1])
    first = fetched_copies(cot_solved, far)
    shares = exchange(copies(exchange(first, FAR), half * near), CLOSE)
    tiles = partial_tiles(shares, slab)
    high, own = reduced(exchange(tiles, "row"), half * far * near)
    needed = exchange(joined(places(sizes), exchange(high, SPREAD), own), "row")
    return tuple(products(needed, cot_direct, solved_panel, scale))


def solution(mesh):
    rows, cols = mesh.devices.shape
    fine = Mesh(mesh.devices.reshape(rows, 2, cols // 16, 2, 2, 2), ("row",) + COL)
    in_specs = (P("row", COL), P(None, ("row",) + COL), P(None, COL), P(None, COL))
    out_specs = (P(None, COL), P("row", COL))
    return jax.shard_map(body, mesh=fine, in_specs=in_specs, out_specs=out_specs, check_vma=False)
```

```python
import jax
import jax.numpy as jnp
from jax import lax
from jax.experimental import pallas as pl
from jax.experimental.pallas import tpu as pltpu
from jax.sharding import PartitionSpec as P

SUB, LANE = 8, 128
F32, BF16 = jnp.float32, jnp.bfloat16
ROW_FIRST, COL_FIRST = 12, 26
PARAMS = pltpu.CompilerParams(vmem_limit_bytes=8 << 20)


def partial_kernel(order, blocks_ref, slab_ref, out_ref):
    where = {c: (q, i) for q, row in enumerate(order) for i, c in enumerate(row)}
    pair = 2
    total = None
    for c in range(0, slab_ref.shape[0], pair):
        left = jnp.concatenate([blocks_ref[where[c + m]] for m in range(pair)], axis=1)
        right = jnp.concatenate([slab_ref[c + m] for m in range(pair)], axis=0)
        term = jnp.dot(left, right, preferred_element_type=F32)
        total = term if total is None else total + term
    across = total.shape[1] // LANE
    for t in range(out_ref.shape[0]):
        i, j = t // across, t % across
        out_ref[t] = total[i * SUB : (i + 1) * SUB, j * LANE : (j + 1) * LANE]


def partial_tiles(order, blocks, slab):
    shares, n, k, b = blocks.shape
    width = slab.shape[-1]
    tiles = (k // SUB) * (width // LANE)

    def kernel(*refs):
        partial_kernel(order, *refs)

    return pl.pallas_call(
        kernel,
        out_shape=jax.ShapeDtypeStruct((tiles, SUB, LANE), F32),
        compiler_params=PARAMS,
        cost_estimate=pl.CostEstimate(
            flops=2 * shares * n * k * b * width, bytes_accessed=2 * (blocks.size + slab.size), transcendentals=0
        ),
    )(blocks, slab)


def reduced_kernel(tiles_ref, high_ref, own_ref):
    pulled = tiles_ref[0]
    for t in range(1, tiles_ref.shape[0]):
        pulled = pulled + tiles_ref[t]
    high = pulled.astype(BF16)
    low = (pulled - high.astype(F32)).astype(BF16)
    for t in range(high_ref.shape[0]):
        high_ref[t] = high
    for t in range(own_ref.shape[0]):
        own_ref[t, 0] = high
        own_ref[t, 1] = low


def reduced(tiles, copies):
    rows = tiles.shape[0]
    tile = tiles.shape[1:]
    return pl.pallas_call(
        reduced_kernel,
        out_shape=[jax.ShapeDtypeStruct((copies,) + tile, BF16), jax.ShapeDtypeStruct((rows, 2) + tile, BF16)],
        compiler_params=PARAMS,
        cost_estimate=pl.CostEstimate(flops=tiles.size, bytes_accessed=10 * tiles.size, transcendentals=0),
    )(tiles)


def product_kernel(scale, tiles_ref, direct_ref, panel_ref, factor_ref, out_ref, left_ref, sum_ref, wide_ref, sems):
    rows, blocks = tiles_ref.shape[0], tiles_ref.shape[1] - 2
    across = direct_ref.shape[1] // LANE
    chunks = sems.shape[0] - 1
    chunk = out_ref.shape[0] // chunks
    for t in range(rows):
        i, j = t // across, t % across
        at = slice(i * SUB, (i + 1) * SUB)
        for b in range(blocks):
            lane = (b * across + j) * LANE
            left_ref[at, lane : lane + LANE] = tiles_ref[t, b].astype(F32)
        lanes = slice(j * LANE, (j + 1) * LANE)
        pulled = tiles_ref[t, blocks].astype(F32) + tiles_ref[t, blocks + 1].astype(F32)
        sum_ref[at, lanes] = (direct_ref[at, lanes].astype(F32) + pulled) * scale
    copies = [pltpu.make_async_copy(sum_ref, factor_ref, sems.at[chunks])]
    copies[0].start()
    for c in range(chunks):
        at = slice(c * chunk, (c + 1) * chunk)
        left = left_ref[:, at].astype(BF16)
        product = lax.dot_general(left, panel_ref[...], (((0,), (0,)), ((), ())), preferred_element_type=F32)
        wide_ref[at] = (product * -scale).astype(BF16)
        copies.append(pltpu.make_async_copy(wide_ref.at[at], out_ref.at[at], sems.at[c]))
        copies[-1].start()
    for copy in copies:
        copy.wait()


def products(tiles, direct, panel, scale):
    k, columns = panel.shape
    depth = (tiles.shape[1] - 2) * direct.shape[1]
    chunks = 4

    def kernel(*refs):
        product_kernel(scale, *refs)

    return pl.pallas_call(
        kernel,
        in_specs=[pl.BlockSpec(memory_space=pltpu.VMEM)] * 3,
        out_specs=[pl.BlockSpec(memory_space=pl.ANY)] * 2,
        out_shape=[jax.ShapeDtypeStruct(direct.shape, F32), jax.ShapeDtypeStruct((depth, columns), BF16)],
        scratch_shapes=[
            pltpu.VMEM((k, depth), F32),
            pltpu.VMEM(direct.shape, F32),
            pltpu.VMEM((depth, columns), BF16),
            pltpu.SemaphoreType.DMA((chunks + 1,)),
        ],
        compiler_params=PARAMS,
        cost_estimate=pl.CostEstimate(
            flops=2 * k * depth * columns, bytes_accessed=2 * (depth * columns + panel.size), transcendentals=0
        ),
    )(tiles, direct, panel)


def copies_kernel(x_ref, out_ref):
    for i in range(out_ref.shape[0]):
        out_ref[i] = x_ref[...]


def fetched_copies_kernel(x_ref, out_ref, sem):
    fetch = pltpu.make_async_copy(x_ref, out_ref.at[0], sem)
    fetch.start()
    fetch.wait()
    for i in range(1, out_ref.shape[0]):
        out_ref[i] = out_ref[0]


def fetched_copies(x, n):
    return pl.pallas_call(
        fetched_copies_kernel,
        in_specs=[pl.BlockSpec(memory_space=pltpu.HBM)],
        out_specs=pl.BlockSpec(memory_space=pltpu.VMEM),
        out_shape=jax.ShapeDtypeStruct((n,) + x.shape, x.dtype),
        scratch_shapes=[pltpu.SemaphoreType.DMA],
        compiler_params=PARAMS,
        cost_estimate=pl.CostEstimate(flops=0, bytes_accessed=4 * n * x.size, transcendentals=0),
    )(pltpu.with_memory_space_constraint(x, pltpu.HBM))


def joined_kernel(order, every_ref, own_ref, out_ref):
    rows, blocks = out_ref.shape[0], out_ref.shape[1] - own_ref.shape[1]
    for t in range(rows):
        for b in range(blocks):
            out_ref[t, b] = every_ref[order[t * blocks + b]]
        out_ref[t, blocks:] = own_ref[t]


def joined(order, every, own):
    rows = own.shape[0]
    blocks = every.shape[0] // rows

    def kernel(*refs):
        joined_kernel(order, *refs)

    shape = (rows, blocks + own.shape[1]) + own.shape[2:]
    return pl.pallas_call(
        kernel,
        out_shape=jax.ShapeDtypeStruct(shape, own.dtype),
        compiler_params=PARAMS,
        cost_estimate=pl.CostEstimate(flops=0, bytes_accessed=4 * (every.size + own.size), transcendentals=0),
    )(every, own)


def copies(x, n):
    return pl.pallas_call(
        copies_kernel,
        out_shape=jax.ShapeDtypeStruct((n,) + x.shape, x.dtype),
        compiler_params=PARAMS,
        cost_estimate=pl.CostEstimate(flops=0, bytes_accessed=2 * (n + 1) * x.size, transcendentals=0),
    )(x)


def reversed_bits(i, bits):
    return sum(((i >> b) & 1) << (bits - 1 - b) for b in range(bits))


def exchange(x, axis, groups):
    return lax.all_to_all(x, axis, 0, 0, tiled=True, axis_index_groups=groups)


def body(inverse_slab, cot_solved, cot_direct, solved_panel):
    scale = 0.5 ** 0.5
    rows, cols = lax.axis_size("row"), lax.axis_size("col")
    halves, nears = 2, 2
    fars = cols // (halves * nears)
    half0, far0, near0 = COL_FIRST // (fars * nears), COL_FIRST // nears % fars, COL_FIRST % nears

    def col(half, far, near):
        return ((half ^ half0) * fars + (far ^ far0)) * nears + (near ^ near0)

    close = [(h, m) for h in range(halves) for m in range(nears)]
    far_groups = [[col(h, f, m) for f in range(fars)] for h, m in close]
    close_groups = [[col(h, f, m) for h, m in close] for f in range(fars)]
    every_col = [COL_FIRST ^ reversed_bits(i, cols.bit_length() - 1) for i in range(cols)]
    every_row = [ROW_FIRST ^ i for i in range(rows)]

    slab = inverse_slab.reshape(cols, cot_solved.shape[1], inverse_slab.shape[1])
    shares = copies(exchange(fetched_copies(cot_solved, fars), "col", far_groups), halves * nears)
    shares = exchange(shares, "col", close_groups)
    tiles = partial_tiles(far_groups, shares, slab)
    high, own = reduced(exchange(tiles, "row", [every_row]), cols)
    every = exchange(high, "col", [every_col])
    needed = [every_col.index(r * (cols // rows) + b) for r in every_row for b in range(cols // rows)]
    tiles = exchange(joined(needed, every, own), "row", [every_row])
    return tuple(products(tiles, cot_direct, solved_panel, scale))


def solution(mesh):
    in_specs = (P("row", "col"), P(None, ("row", "col")), P(None, "col"), P(None, "col"))
    out_specs = (P(None, "col"), P("row", "col"))
    return jax.shard_map(body, mesh=mesh, in_specs=in_specs, out_specs=out_specs, check_vma=False)
```

```python
import jax
import jax.numpy as jnp
from jax import lax
from jax.experimental import pallas as pl
from jax.experimental.pallas import tpu as pltpu
from jax.sharding import PartitionSpec as P

SUB, LANE = 8, 128
F32, BF16 = jnp.float32, jnp.bfloat16
ROW_FIRST, COL_FIRST = 13, 26
PARAMS = pltpu.CompilerParams(vmem_limit_bytes=8 << 20)


def partial_kernel(order, blocks_ref, slab_ref, out_ref):
    where = {c: (q, i) for q, row in enumerate(order) for i, c in enumerate(row)}
    pair = 2
    total = None
    for c in range(0, slab_ref.shape[0], pair):
        left = jnp.concatenate([blocks_ref[where[c + m]] for m in range(pair)], axis=1)
        right = jnp.concatenate([slab_ref[c + m] for m in range(pair)], axis=0)
        term = jnp.dot(left, right, preferred_element_type=F32)
        total = term if total is None else total + term
    across = total.shape[1] // LANE
    for t in range(out_ref.shape[0]):
        i, j = t // across, t % across
        out_ref[t] = total[i * SUB : (i + 1) * SUB, j * LANE : (j + 1) * LANE]


def partial_tiles(order, blocks, slab):
    shares, n, k, b = blocks.shape
    width = slab.shape[-1]
    tiles = (k // SUB) * (width // LANE)

    def kernel(*refs):
        partial_kernel(order, *refs)

    return pl.pallas_call(
        kernel,
        out_shape=jax.ShapeDtypeStruct((tiles, SUB, LANE), F32),
        compiler_params=PARAMS,
        cost_estimate=pl.CostEstimate(
            flops=2 * shares * n * k * b * width, bytes_accessed=2 * (blocks.size + slab.size), transcendentals=0
        ),
    )(blocks, slab)


def reduced_kernel(tiles_ref, high_ref, own_ref):
    pulled = tiles_ref[0]
    for t in range(1, tiles_ref.shape[0]):
        pulled = pulled + tiles_ref[t]
    high = pulled.astype(BF16)
    low = (pulled - high.astype(F32)).astype(BF16)
    for t in range(high_ref.shape[0]):
        high_ref[t] = high
    for t in range(own_ref.shape[0]):
        own_ref[t, 0] = high
        own_ref[t, 1] = low


def reduced(tiles, copies):
    rows = tiles.shape[0]
    tile = tiles.shape[1:]
    return pl.pallas_call(
        reduced_kernel,
        out_shape=[jax.ShapeDtypeStruct((copies,) + tile, BF16), jax.ShapeDtypeStruct((rows, 2) + tile, BF16)],
        compiler_params=PARAMS,
        cost_estimate=pl.CostEstimate(flops=tiles.size, bytes_accessed=10 * tiles.size, transcendentals=0),
    )(tiles)


def product_kernel(scale, tiles_ref, direct_ref, panel_ref, factor_ref, out_ref, left_ref, sum_ref, wide_ref, sems):
    rows, blocks = tiles_ref.shape[0], tiles_ref.shape[1] - 2
    across = direct_ref.shape[1] // LANE
    chunks = sems.shape[0] - 1
    chunk = out_ref.shape[0] // chunks
    for t in range(rows):
        i, j = t // across, t % across
        at = slice(i * SUB, (i + 1) * SUB)
        for b in range(blocks):
            lane = (b * across + j) * LANE
            left_ref[at, lane : lane + LANE] = tiles_ref[t, b].astype(F32)
        lanes = slice(j * LANE, (j + 1) * LANE)
        pulled = tiles_ref[t, blocks].astype(F32) + tiles_ref[t, blocks + 1].astype(F32)
        sum_ref[at, lanes] = (direct_ref[at, lanes].astype(F32) + pulled) * scale
    copies = [pltpu.make_async_copy(sum_ref, factor_ref, sems.at[chunks])]
    copies[0].start()
    for c in range(chunks):
        at = slice(c * chunk, (c + 1) * chunk)
        left = left_ref[:, at].astype(BF16)
        product = lax.dot_general(left, panel_ref[...], (((0,), (0,)), ((), ())), preferred_element_type=F32)
        wide_ref[at] = (product * -scale).astype(BF16)
        copies.append(pltpu.make_async_copy(wide_ref.at[at], out_ref.at[at], sems.at[c]))
        copies[-1].start()
    for copy in copies:
        copy.wait()


def products(tiles, direct, panel, scale):
    k, columns = panel.shape
    depth = (tiles.shape[1] - 2) * direct.shape[1]
    chunks = 4

    def kernel(*refs):
        product_kernel(scale, *refs)

    return pl.pallas_call(
        kernel,
        in_specs=[pl.BlockSpec(memory_space=pltpu.VMEM)] * 3,
        out_specs=[pl.BlockSpec(memory_space=pl.ANY)] * 2,
        out_shape=[jax.ShapeDtypeStruct(direct.shape, F32), jax.ShapeDtypeStruct((depth, columns), BF16)],
        scratch_shapes=[
            pltpu.VMEM((k, depth), F32),
            pltpu.VMEM(direct.shape, F32),
            pltpu.VMEM((depth, columns), BF16),
            pltpu.SemaphoreType.DMA((chunks + 1,)),
        ],
        compiler_params=PARAMS,
        cost_estimate=pl.CostEstimate(
            flops=2 * k * depth * columns, bytes_accessed=2 * (depth * columns + panel.size), transcendentals=0
        ),
    )(tiles, direct, panel)


def copies_kernel(x_ref, out_ref):
    for i in range(out_ref.shape[0]):
        out_ref[i] = x_ref[...]


def fetched_copies_kernel(x_ref, out_ref, sem):
    fetch = pltpu.make_async_copy(x_ref, out_ref.at[0], sem)
    fetch.start()
    fetch.wait()
    for i in range(1, out_ref.shape[0]):
        out_ref[i] = out_ref[0]


def fetched_copies(x, n):
    return pl.pallas_call(
        fetched_copies_kernel,
        in_specs=[pl.BlockSpec(memory_space=pltpu.HBM)],
        out_specs=pl.BlockSpec(memory_space=pltpu.VMEM),
        out_shape=jax.ShapeDtypeStruct((n,) + x.shape, x.dtype),
        scratch_shapes=[pltpu.SemaphoreType.DMA],
        compiler_params=PARAMS,
        cost_estimate=pl.CostEstimate(flops=0, bytes_accessed=4 * n * x.size, transcendentals=0),
    )(pltpu.with_memory_space_constraint(x, pltpu.HBM))


def joined_kernel(order, every_ref, own_ref, out_ref):
    rows, blocks = out_ref.shape[0], out_ref.shape[1] - own_ref.shape[1]
    for t in range(rows):
        for b in range(blocks):
            out_ref[t, b] = every_ref[order[t * blocks + b]]
        out_ref[t, blocks:] = own_ref[t]


def joined(order, every, own):
    rows = own.shape[0]
    blocks = every.shape[0] // rows

    def kernel(*refs):
        joined_kernel(order, *refs)

    shape = (rows, blocks + own.shape[1]) + own.shape[2:]
    return pl.pallas_call(
        kernel,
        out_shape=jax.ShapeDtypeStruct(shape, own.dtype),
        compiler_params=PARAMS,
        cost_estimate=pl.CostEstimate(flops=0, bytes_accessed=4 * (every.size + own.size), transcendentals=0),
    )(every, own)


def copies(x, n):
    return pl.pallas_call(
        copies_kernel,
        out_shape=jax.ShapeDtypeStruct((n,) + x.shape, x.dtype),
        compiler_params=PARAMS,
        cost_estimate=pl.CostEstimate(flops=0, bytes_accessed=2 * (n + 1) * x.size, transcendentals=0),
    )(x)


def reversed_bits(i, bits):
    return sum(((i >> b) & 1) << (bits - 1 - b) for b in range(bits))


def exchange(x, axis, groups):
    return lax.all_to_all(x, axis, 0, 0, tiled=True, axis_index_groups=groups)


def body(inverse_slab, cot_solved, cot_direct, solved_panel):
    scale = 0.5 ** 0.5
    rows, cols = lax.axis_size("row"), lax.axis_size("col")
    halves, nears = 2, 2
    fars = cols // (halves * nears)
    half0, far0, near0 = COL_FIRST // (fars * nears), COL_FIRST // nears % fars, COL_FIRST % nears

    def col(half, far, near):
        return ((half ^ half0) * fars + (far ^ far0)) * nears + (near ^ near0)

    close = [(h, m) for h in range(halves) for m in range(nears)]
    far_groups = [[col(h, f, m) for f in range(fars)] for h, m in close]
    close_groups = [[col(h, f, m) for h, m in close] for f in range(fars)]
    every_col = [COL_FIRST ^ reversed_bits(i, cols.bit_length() - 1) for i in range(cols)]
    every_row = [ROW_FIRST ^ i for i in range(rows)]

    slab = inverse_slab.reshape(cols, cot_solved.shape[1], inverse_slab.shape[1])
    shares = copies(exchange(fetched_copies(cot_solved, fars), "col", far_groups), halves * nears)
    shares = exchange(shares, "col", close_groups)
    tiles = partial_tiles(far_groups, shares, slab)
    high, own = reduced(exchange(tiles, "row", [every_row]), cols)
    every = exchange(high, "col", [every_col])
    needed = [every_col.index(r * (cols // rows) + b) for r in every_row for b in range(cols // rows)]
    tiles = exchange(joined(needed, every, own), "row", [every_row])
    return tuple(products(tiles, cot_direct, solved_panel, scale))


def solution(mesh):
    in_specs = (P("row", "col"), P(None, ("row", "col")), P(None, "col"), P(None, "col"))
    out_specs = (P(None, "col"), P("row", "col"))
    return jax.shard_map(body, mesh=mesh, in_specs=in_specs, out_specs=out_specs, check_vma=False)
```

```python
import jax
import jax.numpy as jnp
from jax import lax
from jax.experimental import pallas as pl
from jax.experimental.pallas import tpu as pltpu
from jax.sharding import PartitionSpec as P

SUB, LANE = 8, 128
F32, BF16 = jnp.float32, jnp.bfloat16
ROW_FIRST, COL_FIRST = 13, 26
PARAMS = pltpu.CompilerParams(vmem_limit_bytes=8 << 20)


def partial_kernel(order, blocks_ref, slab_ref, out_ref):
    where = {c: (q, i) for q, row in enumerate(order) for i, c in enumerate(row)}
    pair = 2
    total = None
    for c in range(0, slab_ref.shape[0], pair):
        left = jnp.concatenate([blocks_ref[where[c + m]] for m in range(pair)], axis=1)
        right = jnp.concatenate([slab_ref[c + m] for m in range(pair)], axis=0)
        term = jnp.dot(left, right, preferred_element_type=F32)
        total = term if total is None else total + term
    across = total.shape[1] // LANE
    for t in range(out_ref.shape[0]):
        i, j = t // across, t % across
        out_ref[t] = total[i * SUB : (i + 1) * SUB, j * LANE : (j + 1) * LANE]


def partial_tiles(order, blocks, slab):
    shares, n, k, b = blocks.shape
    width = slab.shape[-1]
    tiles = (k // SUB) * (width // LANE)

    def kernel(*refs):
        partial_kernel(order, *refs)

    return pl.pallas_call(
        kernel,
        out_shape=jax.ShapeDtypeStruct((tiles, SUB, LANE), F32),
        compiler_params=PARAMS,
        cost_estimate=pl.CostEstimate(
            flops=2 * shares * n * k * b * width, bytes_accessed=2 * (blocks.size + slab.size), transcendentals=0
        ),
    )(blocks, slab)


def reduced_kernel(tiles_ref, high_ref, own_ref):
    pulled = tiles_ref[0]
    for t in range(1, tiles_ref.shape[0]):
        pulled = pulled + tiles_ref[t]
    high = pulled.astype(BF16)
    for t in range(high_ref.shape[0]):
        high_ref[t] = high
    for t in range(own_ref.shape[0]):
        own_ref[t, 0] = high


def reduced(tiles, copies):
    rows = tiles.shape[0]
    tile = tiles.shape[1:]
    return pl.pallas_call(
        reduced_kernel,
        out_shape=[jax.ShapeDtypeStruct((copies,) + tile, BF16), jax.ShapeDtypeStruct((rows, 1) + tile, BF16)],
        compiler_params=PARAMS,
        cost_estimate=pl.CostEstimate(flops=tiles.size, bytes_accessed=10 * tiles.size, transcendentals=0),
    )(tiles)


def product_kernel(scale, tiles_ref, direct_ref, panel_ref, factor_ref, out_ref, left_ref, sum_ref, wide_ref, sems):
    rows, blocks = tiles_ref.shape[0], tiles_ref.shape[1] - 1
    across = direct_ref.shape[1] // LANE
    chunks = sems.shape[0] - 1
    chunk = out_ref.shape[0] // chunks
    for t in range(rows):
        i, j = t // across, t % across
        at = slice(i * SUB, (i + 1) * SUB)
        for b in range(blocks):
            lane = (b * across + j) * LANE
            left_ref[at, lane : lane + LANE] = tiles_ref[t, b].astype(F32)
        lanes = slice(j * LANE, (j + 1) * LANE)
        pulled = tiles_ref[t, blocks].astype(F32)
        sum_ref[at, lanes] = (direct_ref[at, lanes].astype(F32) + pulled) * scale
    copies = [pltpu.make_async_copy(sum_ref, factor_ref, sems.at[chunks])]
    copies[0].start()
    for c in range(chunks):
        at = slice(c * chunk, (c + 1) * chunk)
        left = left_ref[:, at].astype(BF16)
        product = lax.dot_general(left, panel_ref[...], (((0,), (0,)), ((), ())), preferred_element_type=F32)
        wide_ref[at] = (product * -scale).astype(BF16)
        copies.append(pltpu.make_async_copy(wide_ref.at[at], out_ref.at[at], sems.at[c]))
        copies[-1].start()
    for copy in copies:
        copy.wait()


def products(tiles, direct, panel, scale):
    k, columns = panel.shape
    depth = (tiles.shape[1] - 1) * direct.shape[1]
    chunks = 4

    def kernel(*refs):
        product_kernel(scale, *refs)

    return pl.pallas_call(
        kernel,
        in_specs=[pl.BlockSpec(memory_space=pltpu.VMEM)] * 3,
        out_specs=[pl.BlockSpec(memory_space=pl.ANY)] * 2,
        out_shape=[jax.ShapeDtypeStruct(direct.shape, F32), jax.ShapeDtypeStruct((depth, columns), BF16)],
        scratch_shapes=[
            pltpu.VMEM((k, depth), F32),
            pltpu.VMEM(direct.shape, F32),
            pltpu.VMEM((depth, columns), BF16),
            pltpu.SemaphoreType.DMA((chunks + 1,)),
        ],
        compiler_params=PARAMS,
        cost_estimate=pl.CostEstimate(
            flops=2 * k * depth * columns, bytes_accessed=2 * (depth * columns + panel.size), transcendentals=0
        ),
    )(tiles, direct, panel)


def copies_kernel(x_ref, out_ref):
    for i in range(out_ref.shape[0]):
        out_ref[i] = x_ref[...]


def fetched_copies_kernel(x_ref, out_ref, sem):
    fetch = pltpu.make_async_copy(x_ref, out_ref.at[0], sem)
    fetch.start()
    fetch.wait()
    for i in range(1, out_ref.shape[0]):
        out_ref[i] = out_ref[0]


def fetched_copies(x, n):
    return pl.pallas_call(
        fetched_copies_kernel,
        in_specs=[pl.BlockSpec(memory_space=pltpu.HBM)],
        out_specs=pl.BlockSpec(memory_space=pltpu.VMEM),
        out_shape=jax.ShapeDtypeStruct((n,) + x.shape, x.dtype),
        scratch_shapes=[pltpu.SemaphoreType.DMA],
        compiler_params=PARAMS,
        cost_estimate=pl.CostEstimate(flops=0, bytes_accessed=4 * n * x.size, transcendentals=0),
    )(pltpu.with_memory_space_constraint(x, pltpu.HBM))


def joined_kernel(order, every_ref, own_ref, out_ref):
    rows, blocks = out_ref.shape[0], out_ref.shape[1] - own_ref.shape[1]
    for t in range(rows):
        for b in range(blocks):
            out_ref[t, b] = every_ref[order[t * blocks + b]]
        out_ref[t, blocks:] = own_ref[t]


def joined(order, every, own):
    rows = own.shape[0]
    blocks = every.shape[0] // rows

    def kernel(*refs):
        joined_kernel(order, *refs)

    shape = (rows, blocks + own.shape[1]) + own.shape[2:]
    return pl.pallas_call(
        kernel,
        out_shape=jax.ShapeDtypeStruct(shape, own.dtype),
        compiler_params=PARAMS,
        cost_estimate=pl.CostEstimate(flops=0, bytes_accessed=4 * (every.size + own.size), transcendentals=0),
    )(every, own)


def copies(x, n):
    return pl.pallas_call(
        copies_kernel,
        out_shape=jax.ShapeDtypeStruct((n,) + x.shape, x.dtype),
        compiler_params=PARAMS,
        cost_estimate=pl.CostEstimate(flops=0, bytes_accessed=2 * (n + 1) * x.size, transcendentals=0),
    )(x)


def reversed_bits(i, bits):
    return sum(((i >> b) & 1) << (bits - 1 - b) for b in range(bits))


def exchange(x, axis, groups):
    return lax.all_to_all(x, axis, 0, 0, tiled=True, axis_index_groups=groups)


def body(inverse_slab, cot_solved, cot_direct, solved_panel):
    scale = 0.5 ** 0.5
    rows, cols = lax.axis_size("row"), lax.axis_size("col")
    halves, nears = 2, 2
    fars = cols // (halves * nears)
    half0, far0, near0 = COL_FIRST // (fars * nears), COL_FIRST // nears % fars, COL_FIRST % nears

    def col(half, far, near):
        return ((half ^ half0) * fars + (far ^ far0)) * nears + (near ^ near0)

    close = [(h, m) for h in range(halves) for m in range(nears)]
    far_groups = [[col(h, f, m) for f in range(fars)] for h, m in close]
    close_groups = [[col(h, f, m) for h, m in close] for f in range(fars)]
    every_col = [COL_FIRST ^ reversed_bits(i, cols.bit_length() - 1) for i in range(cols)]
    every_row = [ROW_FIRST ^ i for i in range(rows)]

    slab = inverse_slab.reshape(cols, cot_solved.shape[1], inverse_slab.shape[1])
    shares = copies(exchange(fetched_copies(cot_solved, fars), "col", far_groups), halves * nears)
    shares = exchange(shares, "col", close_groups)
    tiles = partial_tiles(far_groups, shares, slab)
    high, own = reduced(exchange(tiles, "row", [every_row]), cols)
    every = exchange(high, "col", [every_col])
    needed = [every_col.index(r * (cols // rows) + b) for r in every_row for b in range(cols // rows)]
    tiles = exchange(joined(needed, every, own), "row", [every_row])
    return tuple(products(tiles, cot_direct, solved_panel, scale))


def solution(mesh):
    in_specs = (P("row", "col"), P(None, ("row", "col")), P(None, "col"), P(None, "col"))
    out_specs = (P(None, "col"), P("row", "col"))
    return jax.shard_map(body, mesh=mesh, in_specs=in_specs, out_specs=out_specs, check_vma=False)
```
